256 devices in a mesh: member: 16 (over y_lo, x, core), tile: 16 (over y_hi, z).
Axes of the slice: x: 4, y: 4 (y_hi: 2, y_lo: 2; y = y_hi * 2 + y_lo), z: 8, core: 2. Of those that a mesh axis runs over, the one named last changes fastest.
Arguments:
- atmos_state: float32 [16, 4, 128, 72, 256], P('member', None, 'tile'), may hold values from -6 to 6
- ocean_slots: float32 [16, 4, 128, 62, 256], P('member', None, 'tile'), may hold values from -6 to 6
- owner_map: int32 [16], P('tile'), may hold values from 0 to 15
- land_mask: int32 [128, 256], P('tile'), may hold values 0 or 1
- transfer_coefficient: float32 [128, 256], P('tile'), may hold values from 0.5 to 2
- air_mixing: float32 [72, 72], replicated, may hold values from -0.75 to 0.75
- sea_mixing: float32 [62, 62], replicated, may hold values from -0.75 to 0.75
Outputs:
- atmos_next: float32 [16, 4, 128, 72, 256], P('member', None, 'tile')
- ocean_next: float32 [16, 4, 128, 62, 256], P('member', None, 'tile')
The draws below stay inside these ranges and needn't reach their ends.
Inputs may be any that keep to these rules, and one draw needn't show every extreme that they name: owner_map[t] is the member whose slot holds tile t's ocean; the other slots of that tile are not read.
All inputs are finite; a program needn't handle non-finite values. No bound on the sum of `land_mask` on one device may be relied on, other than what follows from the above.
Results may differ from the reference program's by a relative error of at most 0.0001.
Values sent between devices are 32-bit elements; how exact they have to be, the bound alone decides.
A program may use at most 64 MiB of HBM per device.

```python
import math
import jax
import jax.numpy as jnp
from jax import lax

LEV = 72
OLEV = 62
ROWS = 8
NLON = 256
NSUB = 4
MEMBERS = 16
NTILES = 16
NLAT = 128


def place_ends(entries, stream_key, low, high):
    place = [jax.random.randint(jax.random.fold_in(stream_key, axis), (), 0, length) for axis, length in enumerate(entries.shape)]
    main_axis = entries.shape.index(max(entries.shape))
    beside = place[:main_axis] + [(place[main_axis] + 1) % entries.shape[main_axis]] + place[main_axis + 1:]
    return entries.at[tuple(place)].set(low).at[tuple(beside)].set(high)


def block_levels(key, shape, cuts, least, largest):
    level, own = 1.0, jax.random.fold_in(key, 6)
    for position, blocks in cuts:
        steps = jnp.exp(jax.random.uniform(jax.random.fold_in(own, position), (blocks,), jnp.float32, least / len(cuts), largest / len(cuts)))
        level = level * jnp.repeat(steps, shape[position] // blocks).reshape([-1 if axis == position else 1 for axis in range(len(shape))])
    return level


def gaussian(stream_key, shape, deviation, reach, shards=(), held_as=jnp.bfloat16):
    values = jax.random.normal(stream_key, shape, jnp.float32) * deviation
    if len(shards) > 0:
        values = block_levels(stream_key, shape, shards, -0.22, 0.18) * values
    return jnp.clip(values, min=-reach, max=reach).astype(held_as)


def setup_inputs(seed: int = 0) -> dict:
    key_list = jax.random.split(jax.random.key(seed), 8)
    atmos_state = gaussian(key_list[0], (MEMBERS, 4, NLAT, LEV, NLON), 1.0, 6.0, ((0, 16), (2, 16)), jnp.float32)
    ocean_slots = gaussian(key_list[1], (MEMBERS, 4, NLAT, OLEV, NLON), 1.0, 6.0, ((0, 16), (2, 16)), jnp.float32)
    owner_map = place_ends(jax.random.randint(key_list[2], (NTILES,), 0, MEMBERS), jax.random.fold_in(key_list[2], 1), 0, MEMBERS - 1).astype(jnp.int32)
    land_mask = place_ends((jax.random.randint(key_list[3], (NLAT, NLON), 0, 10) < 7).astype(jnp.int32), jax.random.fold_in(key_list[3], 1), 0, 1)
    transfer_coefficient = jnp.clip(jnp.exp(math.log(2.0) - 1.3862944 * jax.random.uniform(key_list[4], (NLAT, NLON), jnp.float32) ** block_levels(key_list[4], (NLAT, NLON), ((0, 16),), -0.2, 0.2)), 0.5, 2.0)
    air_mixing = gaussian(key_list[5], (LEV, LEV), LEV ** -0.5, 0.75, (), jnp.float32)
    sea_mixing = gaussian(key_list[6], (OLEV, OLEV), OLEV ** -0.5, 0.75, (), jnp.float32)
    return dict(atmos_state=atmos_state, ocean_slots=ocean_slots, owner_map=owner_map, land_mask=land_mask, transfer_coefficient=transfer_coefficient, air_mixing=air_mixing, sea_mixing=sea_mixing)


DIFFUSE = 0.2
ADVECT_RATE = 0.15
CORIOLIS_MAX = 0.2
AIR_STEP = 0.05
SEA_STEP = 0.25

def coriolis_of(row_index, row_total):
    latitude = math.pi * ((row_index.astype(jnp.float32) + 0.5) / row_total - 0.5)
    return (CORIOLIS_MAX * jnp.sin(latitude)).reshape(-1, 1, 1)

def dynamics(padded, coriolis):
    center = padded[:, 1:-1]
    north_row = padded[:, 2:]
    south_row = padded[:, :-2]
    east_col = jnp.roll(center, -1, axis=3)
    west_col = jnp.roll(center, 1, axis=3)
    laplace = north_row + south_row + east_col + west_col - 4.0 * center
    zonal_diff = 0.5 * (east_col - west_col)
    merid_diff = 0.5 * (north_row - south_row)
    east_wind = center[2]
    north_wind = center[3]
    advect = east_wind * zonal_diff[:2] + north_wind * merid_diff[:2]
    tracers = center[:2] + DIFFUSE * laplace[:2] - ADVECT_RATE * advect
    east_new = east_wind + DIFFUSE * laplace[2] + coriolis * north_wind
    north_new = north_wind + DIFFUSE * laplace[3] - coriolis * east_wind
    return jnp.concatenate([tracers, east_new[None], north_new[None]], axis=0)

def column_mix(fields, mixing):
    moved = jnp.einsum('kl,frlc->frkc', mixing, fields, precision=lax.Precision.HIGHEST)
    return 0.5 * fields + 0.5 * moved

def fluxes(fields, surface):
    east_diff = fields[2, :, 0, :] - surface[1]
    north_diff = fields[3, :, 0, :] - surface[2]
    speed = jnp.sqrt(1.0 + east_diff * east_diff + north_diff * north_diff)
    factor = surface[3] * speed
    return jnp.stack([factor * (surface[0] - fields[0, :, 0, :]), factor * (jnp.tanh(surface[0]) - fields[1, :, 0, :]), factor * east_diff, factor * north_diff])

def window(atmosphere, surface, air_mixing):
    coriolis = coriolis_of(jnp.arange(NLAT), NLAT)
    signs = jnp.array([1.0, 1.0, -1.0, -1.0], jnp.float32)[:, None, None]
    accumulated = jnp.zeros((4, NLAT, NLON), jnp.float32)
    for substep in range(NSUB):
        surface_flux = fluxes(atmosphere, surface)
        padded = jnp.pad(atmosphere, ((0, 0), (1, 1), (0, 0), (0, 0)))
        updated = column_mix(dynamics(padded, coriolis), air_mixing)
        atmosphere = updated.at[:, :, 0, :].add(AIR_STEP * signs * surface_flux)
        accumulated = accumulated + surface_flux
    return (atmosphere, accumulated / NSUB)

def reference(atmos_state, ocean_slots, owner_map, land_mask, transfer_coefficient, air_mixing, sea_mixing):
    owner_row = jnp.repeat(owner_map, ROWS, total_repeat_length=NLAT)
    is_owner = jnp.arange(MEMBERS)[:, None] == owner_row[None, :]
    ocean_block = lax.optimization_barrier(jnp.sum(jnp.where(is_owner[:, None, :, None, None], ocean_slots, 0.0), axis=0))
    weight = transfer_coefficient * land_mask.astype(jnp.float32)
    surface = jnp.stack([ocean_block[0, :, 0, :], ocean_block[2, :, 0, :], ocean_block[3, :, 0, :], weight])
    atmos_next, accumulated = jax.vmap(window, in_axes=(0, None, None))(atmos_state, surface, air_mixing)
    mean_flux = lax.optimization_barrier(jnp.sum(accumulated, axis=0)) / MEMBERS
    forced = ocean_block.at[:, :, 0, :].add(SEA_STEP * mean_flux)
    mixed_ocean = column_mix(forced, sea_mixing)
    stepped = jnp.where(land_mask[None, :, None, :] == 1, mixed_ocean, ocean_block)
    ocean_next = jnp.where(is_owner[:, None, :, None, None], stepped[None], ocean_slots)
    return (atmos_next, ocean_next)
```

```python
import functools

import jax
import jax.numpy as jnp
import numpy as np
from jax import lax
from jax.experimental import pallas as pl
from jax.experimental.pallas import tpu as pltpu
from jax.sharding import PartitionSpec as P

NSUB = 4
DIFFUSE = 0.2
ADVECT_RATE = 0.15
CORIOLIS_MAX = 0.2
AIR_STEP = 0.05
SEA_STEP = 0.25
MESH = pl.DeviceIdType.MESH
SIGNS = (1.0, 1.0, -1.0, -1.0)


def stacked_left(mix, out_ref, pad):
    size = mix.shape[0]
    row = lax.broadcasted_iota(jnp.int32, (size, size), 0)
    col = lax.broadcasted_iota(jnp.int32, (size, size), 1)
    whole = 0.5 * mix + jnp.where(row == col, 0.5, 0.0)
    high = whole.astype(jnp.bfloat16).astype(jnp.float32)
    low = whole - high
    out_ref[...] = jnp.zeros_like(out_ref)
    out_ref[:, 0:size] = high
    out_ref[:, pad : pad + size] = high
    out_ref[:, 2 * pad : 2 * pad + size] = low


def stacked_right(cells, pad):
    size, width = cells.shape
    if pad > size:
        cells = jnp.concatenate([cells, jnp.zeros((pad - size, width), jnp.float32)], axis=0)
    high = cells.astype(jnp.bfloat16)
    low = (cells - high.astype(jnp.float32)).astype(jnp.bfloat16)
    return jnp.concatenate([high, low, high], axis=0)


def coriolis_rows(tile, tiles, rows, width):
    total = rows * tiles
    sin_tile = jnp.float32(0.0)
    cos_tile = jnp.float32(0.0)
    for index in range(tiles):
        angle = np.pi * (index * rows / total - 0.5)
        sin_tile = jnp.where(tile == index, jnp.float32(CORIOLIS_MAX * np.sin(angle)), sin_tile)
        cos_tile = jnp.where(tile == index, jnp.float32(CORIOLIS_MAX * np.cos(angle)), cos_tile)
    line = lax.broadcasted_iota(jnp.int32, (rows, width), 0)
    sin_row = jnp.zeros((rows, width), jnp.float32)
    cos_row = jnp.zeros((rows, width), jnp.float32)
    for index in range(rows):
        angle = np.pi * (index + 0.5) / total
        sin_row = jnp.where(line == index, jnp.float32(np.sin(angle)), sin_row)
        cos_row = jnp.where(line == index, jnp.float32(np.cos(angle)), cos_row)
    return sin_tile * cos_row + cos_tile * sin_row


def mix_levels(left, cells, pad):
    return jnp.dot(left, stacked_right(cells, pad), preferred_element_type=jnp.float32)


def kernel(
    members,
    tiles,
    owner_hbm,
    atm_hbm,
    ocn_hbm,
    mask_hbm,
    coef_hbm,
    air_hbm,
    sea_hbm,
    atm_out,
    ocn_out,
    state,
    halo,
    ocn,
    ocn_mixed,
    ocn_top,
    owner_ref,
    mask,
    coef,
    air,
    sea,
    cor,
    air_f32,
    sea_f32,
    air_left,
    sea_left,
    sea_share,
    top,
    push,
    surf,
    acc,
    part,
    gathered,
    spread,
    load_sem,
    halo_send,
    halo_recv,
    part_send,
    part_recv,
    spread_send,
    spread_recv,
):
    me = lax.axis_index("member")
    tile = lax.axis_index("tile")
    rows, lev, lon = state.shape[2:]
    olev = ocn.shape[2] // rows
    halves = lon // 128
    last_row = rows - 1
    air_pad = -(-lev // 16) * 16
    sea_pad = -(-olev // 16) * 16
    has_south = tile > 0
    has_north = tile < tiles - 1

    barrier = pltpu.get_barrier_semaphore()

    @pl.loop(1, members)
    def _(d):
        pl.semaphore_signal(
            barrier, inc=1, device_id=(lax.rem(me + d, members), tile), device_id_type=MESH
        )

    @pl.when(has_south)
    def _():
        pl.semaphore_signal(barrier, inc=1, device_id=(me, tile - 1), device_id_type=MESH)

    @pl.when(has_north)
    def _():
        pl.semaphore_signal(barrier, inc=1, device_id=(me, tile + 1), device_id_type=MESH)

    loads = [pltpu.make_async_copy(ocn_hbm.at[f, 0:rows], ocn_top.at[i], load_sem.at[i]) for i, f in enumerate((0, 2, 3))]
    loads += [pltpu.make_async_copy(atm_hbm.at[0, f], state.at[0, f], load_sem.at[3 + f]) for f in range(4)]
    loads += [
        pltpu.make_async_copy(mask_hbm, mask, load_sem.at[7]),
        pltpu.make_async_copy(owner_hbm, owner_ref, load_sem.at[8]),
        pltpu.make_async_copy(coef_hbm, coef, load_sem.at[9]),
        pltpu.make_async_copy(air_hbm, air, load_sem.at[10]),
        pltpu.make_async_copy(sea_hbm, sea, load_sem.at[11]),
    ]
    loads += [
        pltpu.make_async_copy(ocn_hbm.at[:, :, pl.ds(128 * h, 128)], ocn.at[:, h], load_sem.at[12 + h])
        for h in range(halves)
    ]
    for load in loads:
        load.start()

    @pl.when(jnp.logical_not(has_south))
    def _():
        @pl.loop(0, NSUB)
        def _(k):
            for f in range(4):
                halo[k, 0, f] = jnp.zeros((lev, lon), jnp.float32)

    @pl.when(jnp.logical_not(has_north))
    def _():
        @pl.loop(0, NSUB)
        def _(k):
            for f in range(4):
                halo[k, 1, f] = jnp.zeros((lev, lon), jnp.float32)

    def to_south(source, k, f):
        return pltpu.make_async_remote_copy(
            src_ref=source,
            dst_ref=halo.at[k, 1, f],
            send_sem=halo_send.at[k, 0, f],
            recv_sem=halo_recv.at[k, 1, f],
            device_id=(me, tile - 1),
            device_id_type=MESH,
        )

    def to_north(source, k, f):
        return pltpu.make_async_remote_copy(
            src_ref=source,
            dst_ref=halo.at[k, 0, f],
            send_sem=halo_send.at[k, 1, f],
            recv_sem=halo_recv.at[k, 0, f],
            device_id=(me, tile + 1),
            device_id_type=MESH,
        )

    block = part.shape[2]

    def pieces():
        for f in range(4):
            for half in range(2):
                for group in range(2):
                    index = (f * 2 + half) * 2 + group
                    place = (index * 4 // block, slice(index * 4 % block, index * 4 % block + 4))
                    yield f, slice(128 * half, 128 * half + 128), slice(4 * group, 4 * group + 4), place

    def part_copy(i, d):
        target = lax.rem(me + d, members)
        return pltpu.make_async_remote_copy(
            src_ref=part.at[i, target],
            dst_ref=gathered.at[i, d - 1],
            send_sem=part_send.at[i],
            recv_sem=part_recv.at[i],
            device_id=(target, tile),
            device_id_type=MESH,
        )

    def spread_copy(i, d):
        target = lax.rem(me + d, members)
        return pltpu.make_async_remote_copy(
            src_ref=spread.at[i, me],
            dst_ref=spread.at[i, me],
            send_sem=spread_send.at[i],
            recv_sem=spread_recv.at[i],
            device_id=(target, tile),
            device_id_type=MESH,
        )

    def all_pieces(ref, i, send, recv):
        whole = ref.at[i, pl.ds(0, members - 1)]
        return pltpu.make_async_remote_copy(
            src_ref=whole,
            dst_ref=whole,
            send_sem=send.at[i],
            recv_sem=recv.at[i],
            device_id=(lax.rem(me + 1, members), tile),
            device_id_type=MESH,
        )

    def sum_start(i, values):
        for f, cols, lines, (slot, at) in pieces():
            part[i, slot, at, :] = values[f][lines, cols]

        @pl.loop(1, members)
        def _(d):
            part_copy(i, d).start()

    def sum_middle(i):
        all_pieces(gathered, i, part_send, part_recv).wait_recv()
        total = part[i, me]
        for d in range(members - 1):
            total = total + gathered[i, d]
        spread[i, me] = total

        @pl.loop(1, members)
        def _(d):
            spread_copy(i, d).start()

    def sum_finish(i, out_ref):
        all_pieces(spread, i, spread_send, spread_recv).wait_recv()
        for f, cols, lines, (slot, at) in pieces():
            out_ref[f, lines, cols] = spread[i, slot, at, :]

    def sum_drain(i):
        all_pieces(gathered, i, part_send, part_recv).wait_send()
        all_pieces(spread, i, spread_send, spread_recv).wait_send()

    for load in loads[:3] + loads[8:9]:
        load.wait()
    owned = jnp.broadcast_to(owner_ref[...], (rows, lon)) == me
    tops = [jnp.where(owned, ocn_top[i], 0.0) for i in range(3)]
    pl.semaphore_wait(
        barrier, members - 1 + has_south.astype(jnp.int32) + has_north.astype(jnp.int32)
    )

    sum_start(0, tops + [jnp.zeros((rows, lon), jnp.float32)])
    for f in range(4):

        @pl.when(has_south)
        def _():
            to_south(atm_hbm.at[0, f, 0], 0, f).start()

        @pl.when(has_north)
        def _():
            to_north(atm_hbm.at[0, f, last_row], 0, f).start()

    for load in loads[9:12]:
        load.wait()
    cor[...] = coriolis_rows(tile, tiles, rows, lon)
    stacked_left(air[...], air_f32, air_pad)
    stacked_left(sea[...], sea_f32, sea_pad)
    air_left[...] = air_f32[...].astype(jnp.bfloat16)
    sea_left[...] = sea_f32[...].astype(jnp.bfloat16)

    for load in loads[3:8] + loads[12:]:
        load.wait()
    for f in range(4):
        top[f] = state[0, f, :, 0, :]
        acc[f] = jnp.zeros((rows, lon), jnp.float32)

    def mix_ocean(f, _):
        for r in range(rows):
            levels = pl.ds(r, olev, stride=rows)
            column = jnp.concatenate([ocn[f, h, levels, :] for h in range(halves)], axis=1)
            column = mix_levels(sea_left[...], column, sea_pad)
            for h in range(halves):
                ocn_mixed[f, h, levels, :] = column[:, 128 * h : 128 * h + 128]
        return _

    sum_middle(0)
    lax.fori_loop(0, 4, mix_ocean, 0)
    sum_finish(0, surf)
    surf[3] = coef[...] * mask[...].astype(jnp.float32)

    def fluxes():
        east = top[2] - surf[1]
        north = top[3] - surf[2]
        factor = surf[3] * jnp.sqrt(1.0 + east * east + north * north)
        values = [
            factor * (surf[0] - top[0]),
            factor * (jnp.tanh(surf[0]) - top[1]),
            factor * east,
            factor * north,
        ]
        for f in range(4):
            acc[f] = acc[f] + values[f]
            push[f] = (AIR_STEP * SIGNS[f]) * values[f]

    def advance(k, f, r, target):
        center = state[k, f, r]
        south = halo[k, 0, f] if r == 0 else state[k, f, r - 1]
        north = halo[k, 1, f] if r == last_row else state[k, f, r + 1]
        east = pltpu.roll(center, lon - 1, 1)
        west = pltpu.roll(center, 1, 1)
        spread_out = DIFFUSE * ((north + south) + (east + west)) + (1.0 - 4.0 * DIFFUSE) * center
        if f < 2:
            flow = state[k, 2, r] * (east - west) + state[k, 3, r] * (north - south)
            moved = spread_out - (0.5 * ADVECT_RATE) * flow
        else:
            turn = cor[r : r + 1, :]
            turn = turn if f == 2 else -turn
            moved = spread_out + turn * state[k, 5 - f, r]
        mixed = mix_levels(air_left[...], moved, air_pad)
        surface = mixed[0:1, :] + push[f, r : r + 1, :]
        target[f, r] = mixed
        target[f, r, 0:1, :] = surface
        top[f, r : r + 1, :] = surface

    def step(k, target, final):
        fluxes()
        if final:
            sum_start(1, [acc[f] for f in range(4)])
        for f in range(4):

            @pl.when(has_south)
            def _():
                to_north(atm_hbm.at[0, f, 0], k, f).wait_recv()

            @pl.when(has_north)
            def _():
                to_south(atm_hbm.at[0, f, 0], k, f).wait_recv()

            advance(k, f, 0, target)
            advance(k, f, last_row, target)
            if not final:

                @pl.when(has_south)
                def _():
                    to_south(target.at[f, 0], k + 1, f).start()

                @pl.when(has_north)
                def _():
                    to_north(target.at[f, last_row], k + 1, f).start()

            for r in range(1, last_row):
                advance(k, f, r, target)
            if final and f == 1:
                sum_middle(1)

    def steps(k, carry):
        step(k, state.at[k + 1], False)
        return carry

    lax.fori_loop(0, NSUB - 1, steps, 0)
    step(NSUB - 1, atm_out.at[0], True)

    sum_finish(1, acc)
    line = lax.broadcasted_iota(jnp.int32, (olev, 1), 0)
    share = SEA_STEP / (NSUB * members) * (0.5 * sea[:, 0:1] + jnp.where(line == 0, 0.5, 0.0))
    sea_share[...] = jnp.broadcast_to(share, (olev, 128))
    wet = jnp.logical_and(owned, mask[...] == 1)

    def finish_ocean(f, carry):
        forcing = acc[f]
        for level in range(olev):
            at = slice(level * rows, level * rows + rows)
            for h in range(halves):
                cols = slice(128 * h, 128 * h + 128)
                stepped = ocn_mixed[f, h, at, :] + sea_share[level : level + 1, :] * forcing[:, cols]
                ocn_out[f, at, cols] = jnp.where(wet[:, cols], stepped, ocn[f, h, at, :])
        return carry

    lax.fori_loop(0, 4, finish_ocean, 0)

    for i in range(2):
        sum_drain(i)

    @pl.loop(0, NSUB)
    def _(k):
        for f in range(4):

            @pl.when(has_south)
            def _():
                to_south(atm_hbm.at[0, f, 0], k, f).wait_send()

            @pl.when(has_north)
            def _():
                to_north(atm_hbm.at[0, f, 0], k, f).wait_send()


def shards(members, tiles, atmos_state, ocean_slots, owner_map, land_mask, transfer, air_mixing, sea_mixing):
    fields, rows, lev, lon = atmos_state.shape[1:]
    olev = ocean_slots.shape[3]
    air_pad = -(-lev // 16) * 16
    sea_pad = -(-olev // 16) * 16
    block = fields * rows * lon // 128 // members
    anywhere = pl.BlockSpec(memory_space=pltpu.MemorySpace.HBM)
    slots = ocean_slots.transpose(0, 1, 3, 2, 4).reshape(fields, olev * rows, lon)
    vmem = pl.BlockSpec(memory_space=pltpu.VMEM)
    atmos, ocean = pl.pallas_call(
        functools.partial(kernel, members, tiles),
        out_shape=(
            jax.ShapeDtypeStruct(atmos_state.shape, jnp.float32),
            jax.ShapeDtypeStruct(slots.shape, jnp.float32),
        ),
        in_specs=[anywhere] * 7,
        out_specs=(vmem, vmem),
        scratch_shapes=[
            pltpu.VMEM((NSUB, fields, rows, lev, lon), jnp.float32),
            pltpu.VMEM((NSUB, 2, fields, lev, lon), jnp.float32),
            pltpu.VMEM((fields, lon // 128, olev * rows, 128), jnp.float32),
            pltpu.VMEM((fields, lon // 128, olev * rows, 128), jnp.float32),
            pltpu.VMEM((3, rows, lon), jnp.float32),
            pltpu.VMEM((1, 1), jnp.int32),
            pltpu.VMEM((rows, lon), jnp.int32),
            pltpu.VMEM((rows, lon), jnp.float32),
            pltpu.VMEM((lev, lev), jnp.float32),
            pltpu.VMEM((olev, olev), jnp.float32),
            pltpu.VMEM((rows, lon), jnp.float32),
            pltpu.VMEM((lev, 3 * air_pad), jnp.float32),
            pltpu.VMEM((olev, 3 * sea_pad), jnp.float32),
            pltpu.VMEM((lev, 3 * air_pad), jnp.bfloat16),
            pltpu.VMEM((olev, 3 * sea_pad), jnp.bfloat16),
            pltpu.VMEM((olev, 128), jnp.float32),
            pltpu.VMEM((fields, rows, lon), jnp.float32),
            pltpu.VMEM((fields, rows, lon), jnp.float32),
            pltpu.VMEM((fields, rows, lon), jnp.float32),
            pltpu.VMEM((fields, rows, lon), jnp.float32),
            pltpu.VMEM((2, members, block, 128), jnp.float32),
            pltpu.VMEM((2, members - 1, block, 128), jnp.float32),
            pltpu.VMEM((2, members, block, 128), jnp.float32),
            pltpu.SemaphoreType.DMA((12 + lon // 128,)),
            pltpu.SemaphoreType.DMA((NSUB, 2, fields)),
            pltpu.SemaphoreType.DMA((NSUB, 2, fields)),
            pltpu.SemaphoreType.DMA((2,)),
            pltpu.SemaphoreType.DMA((2,)),
            pltpu.SemaphoreType.DMA((2,)),
            pltpu.SemaphoreType.DMA((2,)),
        ],
        compiler_params=pltpu.CompilerParams(
            collective_id=0, has_side_effects=True, vmem_limit_bytes=40 * 1024 * 1024
        ),
        name="window",
    )(
        owner_map.reshape(1, 1),
        *[
            pltpu.with_memory_space_constraint(x, pltpu.MemorySpace.HBM)
            for x in (atmos_state, slots, land_mask, transfer, air_mixing, sea_mixing)
        ],
    )
    ocean = ocean.reshape(1, fields, olev, rows, lon).transpose(0, 1, 3, 2, 4)
    return atmos, ocean


def solution(mesh):
    placed = (
        P("member", None, "tile", None, None),
        P("member", None, "tile", None, None),
        P("tile"),
        P("tile", None),
        P("tile", None),
        P(),
        P(),
    )
    return jax.shard_map(
        functools.partial(shards, mesh.shape["member"], mesh.shape["tile"]),
        mesh=mesh,
        in_specs=placed,
        out_specs=(P("member", None, "tile", None, None), P("member", None, "tile", None, None)),
        check_vma=False,
    )
```

```python
import functools

import jax
import jax.numpy as jnp
import numpy as np
from jax import lax
from jax.experimental import pallas as pl
from jax.experimental.pallas import tpu as pltpu
from jax.sharding import PartitionSpec as P

NSUB = 4
DIFFUSE = 0.2
ADVECT_RATE = 0.15
CORIOLIS_MAX = 0.2
AIR_STEP = 0.05
SEA_STEP = 0.25
MESH = pl.DeviceIdType.MESH
SIGNS = (1.0, 1.0, -1.0, -1.0)


def stacked_left(mix, out_ref, pad):
    size = mix.shape[0]
    row = lax.broadcasted_iota(jnp.int32, (size, size), 0)
    col = lax.broadcasted_iota(jnp.int32, (size, size), 1)
    whole = 0.5 * mix + jnp.where(row == col, 0.5, 0.0)
    high = whole.astype(jnp.bfloat16).astype(jnp.float32)
    low = whole - high
    out_ref[...] = jnp.zeros_like(out_ref)
    out_ref[:, 0:size] = high
    out_ref[:, pad : pad + size] = high
    out_ref[:, 2 * pad : 2 * pad + size] = low


def stacked_right(cells, pad):
    size, width = cells.shape
    if pad > size:
        cells = jnp.concatenate([cells, jnp.zeros((pad - size, width), jnp.float32)], axis=0)
    high = cells.astype(jnp.bfloat16)
    low = (cells - high.astype(jnp.float32)).astype(jnp.bfloat16)
    return jnp.concatenate([high, low, high], axis=0)


def coriolis_rows(tile, tiles, rows, width):
    total = rows * tiles
    sin_tile = jnp.float32(0.0)
    cos_tile = jnp.float32(0.0)
    for index in range(tiles):
        angle = np.pi * (index * rows / total - 0.5)
        sin_tile = jnp.where(tile == index, jnp.float32(CORIOLIS_MAX * np.sin(angle)), sin_tile)
        cos_tile = jnp.where(tile == index, jnp.float32(CORIOLIS_MAX * np.cos(angle)), cos_tile)
    line = lax.broadcasted_iota(jnp.int32, (rows, width), 0)
    sin_row = jnp.zeros((rows, width), jnp.float32)
    cos_row = jnp.zeros((rows, width), jnp.float32)
    for index in range(rows):
        angle = np.pi * (index + 0.5) / total
        sin_row = jnp.where(line == index, jnp.float32(np.sin(angle)), sin_row)
        cos_row = jnp.where(line == index, jnp.float32(np.cos(angle)), cos_row)
    return sin_tile * cos_row + cos_tile * sin_row


def mix_levels(left, cells, pad):
    return jnp.dot(left, stacked_right(cells, pad), preferred_element_type=jnp.float32)


def kernel(
    members,
    tiles,
    owner_hbm,
    atm_hbm,
    ocn_hbm,
    mask_hbm,
    coef_hbm,
    air_hbm,
    sea_hbm,
    atm_out,
    ocn,
    sea_share,
    forcing,
    state,
    halo,
    ocn_top,
    owner_ref,
    mask,
    coef,
    air,
    sea,
    cor,
    air_f32,
    sea_f32,
    air_left,
    sea_left,
    top,
    push,
    surf,
    acc,
    part,
    gathered,
    spread,
    load_sem,
    halo_send,
    halo_recv,
    part_send,
    part_recv,
    spread_send,
    spread_recv,
):
    me = lax.axis_index("member")
    tile = lax.axis_index("tile")
    rows, lev, lon = state.shape[2:]
    olev = ocn.shape[2] // rows
    halves = lon // 128
    last_row = rows - 1
    air_pad = -(-lev // 16) * 16
    sea_pad = -(-olev // 16) * 16
    has_south = tile > 0
    has_north = tile < tiles - 1

    barrier = pltpu.get_barrier_semaphore()

    @pl.loop(1, members)
    def _(d):
        pl.semaphore_signal(
            barrier, inc=1, device_id=(lax.rem(me + d, members), tile), device_id_type=MESH
        )

    @pl.when(has_south)
    def _():
        pl.semaphore_signal(barrier, inc=1, device_id=(me, tile - 1), device_id_type=MESH)

    @pl.when(has_north)
    def _():
        pl.semaphore_signal(barrier, inc=1, device_id=(me, tile + 1), device_id_type=MESH)

    loads = [pltpu.make_async_copy(ocn_hbm.at[f, 0:rows], ocn_top.at[i], load_sem.at[i]) for i, f in enumerate((0, 2, 3))]
    loads += [pltpu.make_async_copy(atm_hbm.at[0, f], state.at[0, f], load_sem.at[3 + f]) for f in range(4)]
    loads += [
        pltpu.make_async_copy(mask_hbm, mask, load_sem.at[7]),
        pltpu.make_async_copy(owner_hbm, owner_ref, load_sem.at[8]),
        pltpu.make_async_copy(coef_hbm, coef, load_sem.at[9]),
        pltpu.make_async_copy(air_hbm, air, load_sem.at[10]),
        pltpu.make_async_copy(sea_hbm, sea, load_sem.at[11]),
    ]
    loads += [
        pltpu.make_async_copy(ocn_hbm.at[:, :, pl.ds(128 * h, 128)], ocn.at[:, h], load_sem.at[12 + h])
        for h in range(halves)
    ]
    for load in loads:
        load.start()

    def to_south(source, k, f):
        return pltpu.make_async_remote_copy(
            src_ref=source,
            dst_ref=halo.at[k, 1, f],
            send_sem=halo_send.at[k, 0, f],
            recv_sem=halo_recv.at[k, 1, f],
            device_id=(me, tile - 1),
            device_id_type=MESH,
        )

    def to_north(source, k, f):
        return pltpu.make_async_remote_copy(
            src_ref=source,
            dst_ref=halo.at[k, 0, f],
            send_sem=halo_send.at[k, 1, f],
            recv_sem=halo_recv.at[k, 0, f],
            device_id=(me, tile + 1),
            device_id_type=MESH,
        )

    block = part.shape[2]

    def pieces():
        for f in range(4):
            for half in range(2):
                for group in range(2):
                    index = (f * 2 + half) * 2 + group
                    place = (index * 4 // block, slice(index * 4 % block, index * 4 % block + 4))
                    yield f, slice(128 * half, 128 * half + 128), slice(4 * group, 4 * group + 4), place

    def part_copy(i, d):
        target = lax.rem(me + d, members)
        return pltpu.make_async_remote_copy(
            src_ref=part.at[i, target],
            dst_ref=gathered.at[i, d - 1],
            send_sem=part_send.at[i],
            recv_sem=part_recv.at[i],
            device_id=(target, tile),
            device_id_type=MESH,
        )

    def spread_copy(i, d):
        target = lax.rem(me + d, members)
        return pltpu.make_async_remote_copy(
            src_ref=spread.at[i, me],
            dst_ref=spread.at[i, me],
            send_sem=spread_send.at[i],
            recv_sem=spread_recv.at[i],
            device_id=(target, tile),
            device_id_type=MESH,
        )

    def all_pieces(ref, i, send, recv):
        whole = ref.at[i, pl.ds(0, members - 1)]
        return pltpu.make_async_remote_copy(
            src_ref=whole,
            dst_ref=whole,
            send_sem=send.at[i],
            recv_sem=recv.at[i],
            device_id=(lax.rem(me + 1, members), tile),
            device_id_type=MESH,
        )

    def sum_start(i, values):
        for f, cols, lines, (slot, at) in pieces():
            part[i, slot, at, :] = values[f][lines, cols]

        @pl.loop(1, members)
        def _(d):
            part_copy(i, d).start()

    def sum_middle(i):
        all_pieces(gathered, i, part_send, part_recv).wait_recv()
        total = part[i, me]
        for d in range(members - 1):
            total = total + gathered[i, d]
        spread[i, me] = total

        @pl.loop(1, members)
        def _(d):
            spread_copy(i, d).start()

    def sum_finish(i, out_ref, fields):
        all_pieces(spread, i, spread_send, spread_recv).wait_recv()
        for f, cols, lines, (slot, at) in pieces():
            if f < fields:
                out_ref[f, lines, cols] = spread[i, slot, at, :]

    def sum_drain(i):
        all_pieces(gathered, i, part_send, part_recv).wait_send()
        all_pieces(spread, i, spread_send, spread_recv).wait_send()

    for load in loads[:3] + loads[8:9]:
        load.wait()
    owned = jnp.broadcast_to(owner_ref[...], (rows, lon)) == me
    tops = [jnp.where(owned, ocn_top[i], 0.0) for i in range(3)]
    pl.semaphore_wait(
        barrier, members - 1 + has_south.astype(jnp.int32) + has_north.astype(jnp.int32)
    )

    sum_start(0, tops + [jnp.zeros((rows, lon), jnp.float32)])
    for f in range(4):

        @pl.when(has_south)
        def _():
            to_south(atm_hbm.at[0, f, 0], 0, f).start()

        @pl.when(has_north)
        def _():
            to_north(atm_hbm.at[0, f, last_row], 0, f).start()

    @pl.when(jnp.logical_not(has_south))
    def _():
        @pl.loop(0, NSUB)
        def _(k):
            for f in range(4):
                halo[k, 0, f] = jnp.zeros((lev, lon), jnp.float32)

    @pl.when(jnp.logical_not(has_north))
    def _():
        @pl.loop(0, NSUB)
        def _(k):
            for f in range(4):
                halo[k, 1, f] = jnp.zeros((lev, lon), jnp.float32)

    for load in loads[9:12]:
        load.wait()
    cor[...] = coriolis_rows(tile, tiles, rows, lon)
    stacked_left(air[...], air_f32, air_pad)
    stacked_left(sea[...], sea_f32, sea_pad)
    air_left[...] = air_f32[...].astype(jnp.bfloat16)
    sea_left[...] = sea_f32[...].astype(jnp.bfloat16)

    def fluxes():
        east = top[2] - surf[1]
        north = top[3] - surf[2]
        factor = surf[3] * jnp.sqrt(1.0 + east * east + north * north)
        values = [
            factor * (surf[0] - top[0]),
            factor * (jnp.tanh(surf[0]) - top[1]),
            factor * east,
            factor * north,
        ]
        for f in range(4):
            acc[f] = acc[f] + values[f]
            push[f] = (AIR_STEP * SIGNS[f]) * values[f]

    def advance(k, f, r, target, pushed):
        center = state[k, f, r]
        south = halo[k, 0, f] if r == 0 else state[k, f, r - 1]
        north = halo[k, 1, f] if r == last_row else state[k, f, r + 1]
        east = pltpu.roll(center, lon - 1, 1)
        west = pltpu.roll(center, 1, 1)
        spread_out = DIFFUSE * ((north + south) + (east + west)) + (1.0 - 4.0 * DIFFUSE) * center
        if f < 2:
            flow = state[k, 2, r] * (east - west) + state[k, 3, r] * (north - south)
            moved = spread_out - (0.5 * ADVECT_RATE) * flow
        else:
            turn = cor[r : r + 1, :]
            turn = turn if f == 2 else -turn
            moved = spread_out + turn * state[k, 5 - f, r]
        mixed = mix_levels(air_left[...], moved, air_pad)
        target[f, r] = mixed
        if pushed:
            push_row(f, r, target, mixed[0:1, :])

    def push_row(f, r, target, line):
        surface = line + push[f, r : r + 1, :]
        target[f, r, 0:1, :] = surface
        top[f, r : r + 1, :] = surface

    def interior(k, f, target, pushed):
        for r in range(1, last_row):
            advance(k, f, r, target, pushed)

    def boundary(k, f, target, pushed):
        @pl.when(has_south)
        def _():
            to_north(atm_hbm.at[0, f, 0], k, f).wait_recv()

        @pl.when(has_north)
        def _():
            to_south(atm_hbm.at[0, f, 0], k, f).wait_recv()

        advance(k, f, 0, target, pushed)
        advance(k, f, last_row, target, pushed)

    def send(k, f, target):
        @pl.when(has_south)
        def _():
            to_south(target.at[f, 0], k, f).start()

        @pl.when(has_north)
        def _():
            to_north(target.at[f, last_row], k, f).start()

    for load in loads[3:7]:
        load.wait()
    for f in range(4):
        top[f] = state[0, f, :, 0, :]
        acc[f] = jnp.zeros((rows, lon), jnp.float32)
    first = state.at[1]
    for f in range(4):
        interior(0, f, first, False)
    sum_middle(0)

    for load in loads[7:8] + loads[12:]:
        load.wait()
    wet = jnp.logical_and(owned, mask[...] == 1)
    push[0] = jnp.where(wet, 1.0, 0.0)

    def mix_ocean(f, carry):
        for r in range(rows):
            levels = pl.ds(r, olev, stride=rows)
            column = jnp.concatenate([ocn[f, h, levels, :] for h in range(halves)], axis=1)
            mixed = mix_levels(sea_left[...], column, sea_pad)
            chosen = jnp.broadcast_to(push[0, r : r + 1, :], (olev, lon)) > 0.5
            column = jnp.where(chosen, mixed, column)
            for h in range(halves):
                ocn[f, h, levels, :] = column[:, 128 * h : 128 * h + 128]
        return carry

    lax.fori_loop(0, 4, mix_ocean, 0)
    line = lax.broadcasted_iota(jnp.int32, (olev, 1), 0)
    share = SEA_STEP / (NSUB * members) * (0.5 * sea[:, 0:1] + jnp.where(line == 0, 0.5, 0.0))
    sea_share[...] = jnp.broadcast_to(share, (olev, 128))

    boundary(0, 0, first, False)
    boundary(0, 1, first, False)
    surf[3] = coef[...] * mask[...].astype(jnp.float32)
    sum_finish(0, surf, 3)
    fluxes()
    for f in range(4):
        if f >= 2:
            boundary(0, f, first, False)
        for r in (0, last_row):
            push_row(f, r, first, first[f, r, 0:1, :])
        send(1, f, first)
    for f in range(4):
        for r in range(1, last_row):
            push_row(f, r, first, first[f, r, 0:1, :])

    def middle(k, carry):
        target = state.at[k + 1]
        fluxes()
        for f in range(4):
            interior(k, f, target, True)
            boundary(k, f, target, True)
            send(k + 1, f, target)
        return carry

    lax.fori_loop(1, NSUB - 1, middle, 0)

    last = atm_out.at[0]
    fluxes()
    sum_start(1, [acc[f] for f in range(4)])
    for f in range(4):
        interior(NSUB - 1, f, last, True)
        boundary(NSUB - 1, f, last, True)
        if f == 1:
            sum_middle(1)

    sum_finish(1, acc, 4)

    for f in range(4):
        forcing[f] = jnp.where(wet, acc[f], 0.0)

    for i in range(2):
        sum_drain(i)

    @pl.loop(0, NSUB)
    def _(k):
        for f in range(4):

            @pl.when(has_south)
            def _():
                to_south(atm_hbm.at[0, f, 0], k, f).wait_send()

            @pl.when(has_north)
            def _():
                to_north(atm_hbm.at[0, f, 0], k, f).wait_send()


def put(atmos, base, share, forcing, atmos_out, ocean_out, ocean, sem):
    fields, halves, lines, _ = base.shape
    rows = forcing.shape[1]
    copies = [pltpu.make_async_copy(atmos.at[0, f], atmos_out.at[0, f], sem.at[f]) for f in range(fields)]
    for copy in copies:
        copy.start()
    for f in range(fields):
        for h in range(halves):
            cols = slice(128 * h, 128 * h + 128)
            flux = forcing[f, :, cols]
            for level in range(lines // rows):
                at = slice(level * rows, level * rows + rows)
                ocean[f, h, at, :] = base[f, h, at, :] + share[level : level + 1, :] * flux
            copy = pltpu.make_async_copy(
                ocean.at[f, h], ocean_out.at[f, :, pl.ds(128 * h, 128)], sem.at[fields + f * halves + h]
            )
            copy.start()
            copies.append(copy)
    for copy in copies:
        copy.wait()


def shards(members, tiles, atmos_state, ocean_slots, owner_map, land_mask, transfer, air_mixing, sea_mixing):
    fields, rows, lev, lon = atmos_state.shape[1:]
    olev = ocean_slots.shape[3]
    air_pad = -(-lev // 16) * 16
    sea_pad = -(-olev // 16) * 16
    block = fields * rows * lon // 128 // members
    anywhere = pl.BlockSpec(memory_space=pltpu.MemorySpace.HBM)
    slots = ocean_slots.transpose(0, 1, 3, 2, 4).reshape(fields, olev * rows, lon)
    vmem = pl.BlockSpec(memory_space=pltpu.VMEM)
    halves = lon // 128
    base_shape = (fields, halves, olev * rows, 128)
    atmos, base, share, forcing = pl.pallas_call(
        functools.partial(kernel, members, tiles),
        out_shape=(
            jax.ShapeDtypeStruct(atmos_state.shape, jnp.float32),
            jax.ShapeDtypeStruct(base_shape, jnp.float32),
            jax.ShapeDtypeStruct((olev, 128), jnp.float32),
            jax.ShapeDtypeStruct((fields, rows, lon), jnp.float32),
        ),
        in_specs=[anywhere] * 7,
        out_specs=(vmem,) * 4,
        scratch_shapes=[
            pltpu.VMEM((NSUB, fields, rows, lev, lon), jnp.float32),
            pltpu.VMEM((NSUB, 2, fields, lev, lon), jnp.float32),
            pltpu.VMEM((3, rows, lon), jnp.float32),
            pltpu.VMEM((1, 1), jnp.int32),
            pltpu.VMEM((rows, lon), jnp.int32),
            pltpu.VMEM((rows, lon), jnp.float32),
            pltpu.VMEM((lev, lev), jnp.float32),
            pltpu.VMEM((olev, olev), jnp.float32),
            pltpu.VMEM((rows, lon), jnp.float32),
            pltpu.VMEM((lev, 3 * air_pad), jnp.float32),
            pltpu.VMEM((olev, 3 * sea_pad), jnp.float32),
            pltpu.VMEM((lev, 3 * air_pad), jnp.bfloat16),
            pltpu.VMEM((olev, 3 * sea_pad), jnp.bfloat16),
            pltpu.VMEM((fields, rows, lon), jnp.float32),
            pltpu.VMEM((fields, rows, lon), jnp.float32),
            pltpu.VMEM((fields, rows, lon), jnp.float32),
            pltpu.VMEM((fields, rows, lon), jnp.float32),
            pltpu.VMEM((2, members, block, 128), jnp.float32),
            pltpu.VMEM((2, members - 1, block, 128), jnp.float32),
            pltpu.VMEM((2, members, block, 128), jnp.float32),
            pltpu.SemaphoreType.DMA((12 + lon // 128,)),
            pltpu.SemaphoreType.DMA((NSUB, 2, fields)),
            pltpu.SemaphoreType.DMA((NSUB, 2, fields)),
            pltpu.SemaphoreType.DMA((2,)),
            pltpu.SemaphoreType.DMA((2,)),
            pltpu.SemaphoreType.DMA((2,)),
            pltpu.SemaphoreType.DMA((2,)),
        ],
        compiler_params=pltpu.CompilerParams(
            collective_id=0, has_side_effects=True, vmem_limit_bytes=40 * 1024 * 1024
        ),
        name="window",
    )(
        owner_map.reshape(1, 1),
        *[
            pltpu.with_memory_space_constraint(x, pltpu.MemorySpace.HBM)
            for x in (atmos_state, slots, land_mask, transfer, air_mixing, sea_mixing)
        ],
    )
    atmos, ocean = pl.pallas_call(
        put,
        out_shape=(
            jax.ShapeDtypeStruct(atmos_state.shape, jnp.float32),
            jax.ShapeDtypeStruct(slots.shape, jnp.float32),
        ),
        in_specs=[vmem] * 4,
        out_specs=(anywhere, anywhere),
        scratch_shapes=[
            pltpu.VMEM(base_shape, jnp.float32),
            pltpu.SemaphoreType.DMA((fields * (1 + halves),)),
        ],
        compiler_params=pltpu.CompilerParams(vmem_limit_bytes=8 * 1024 * 1024),
        name="put",
    )(atmos, base, share, forcing)
    ocean = ocean.reshape(1, fields, olev, rows, lon).transpose(0, 1, 3, 2, 4)
    return atmos, ocean


def solution(mesh):
    placed = (
        P("member", None, "tile", None, None),
        P("member", None, "tile", None, None),
        P("tile"),
        P("tile", None),
        P("tile", None),
        P(),
        P(),
    )
    return jax.shard_map(
        functools.partial(shards, mesh.shape["member"], mesh.shape["tile"]),
        mesh=mesh,
        in_specs=placed,
        out_specs=(P("member", None, "tile", None, None), P("member", None, "tile", None, None)),
        check_vma=False,
    )
```

```python
import functools

import jax
import jax.numpy as jnp
import numpy as np
from jax import lax
from jax.experimental import pallas as pl
from jax.experimental.pallas import tpu as pltpu
from jax.sharding import PartitionSpec as P

NSUB = 4
DIFFUSE = 0.2
ADVECT_RATE = 0.15
CORIOLIS_MAX = 0.2
AIR_STEP = 0.05
SEA_STEP = 0.25
MESH = pl.DeviceIdType.MESH
SIGNS = (1.0, 1.0, -1.0, -1.0)


def stacked_left(mix, out_ref, pad):
    size = mix.shape[0]
    row = lax.broadcasted_iota(jnp.int32, (size, size), 0)
    col = lax.broadcasted_iota(jnp.int32, (size, size), 1)
    whole = 0.5 * mix + jnp.where(row == col, 0.5, 0.0)
    high = whole.astype(jnp.bfloat16).astype(jnp.float32)
    low = whole - high
    out_ref[...] = jnp.zeros_like(out_ref)
    out_ref[:, 0:size] = high
    out_ref[:, pad : pad + size] = high
    out_ref[:, 2 * pad : 2 * pad + size] = low


def stacked_right(cells, pad):
    size, width = cells.shape
    if pad > size:
        cells = jnp.concatenate([cells, jnp.zeros((pad - size, width), jnp.float32)], axis=0)
    high = cells.astype(jnp.bfloat16)
    low = (cells - high.astype(jnp.float32)).astype(jnp.bfloat16)
    return jnp.concatenate([high, low, high], axis=0)


def coriolis_rows(tile, tiles, rows, width):
    total = rows * tiles
    sin_tile = jnp.float32(0.0)
    cos_tile = jnp.float32(0.0)
    for index in range(tiles):
        angle = np.pi * (index * rows / total - 0.5)
        sin_tile = jnp.where(tile == index, jnp.float32(CORIOLIS_MAX * np.sin(angle)), sin_tile)
        cos_tile = jnp.where(tile == index, jnp.float32(CORIOLIS_MAX * np.cos(angle)), cos_tile)
    line = lax.broadcasted_iota(jnp.int32, (rows, width), 0)
    sin_row = jnp.zeros((rows, width), jnp.float32)
    cos_row = jnp.zeros((rows, width), jnp.float32)
    for index in range(rows):
        angle = np.pi * (index + 0.5) / total
        sin_row = jnp.where(line == index, jnp.float32(np.sin(angle)), sin_row)
        cos_row = jnp.where(line == index, jnp.float32(np.cos(angle)), cos_row)
    return sin_tile * cos_row + cos_tile * sin_row


def mix_levels(left, cells, pad):
    return jnp.dot(left, stacked_right(cells, pad), preferred_element_type=jnp.float32)


def kernel(
    members,
    tiles,
    owner_hbm,
    atm_hbm,
    ocn_hbm,
    mask_hbm,
    coef_hbm,
    air_hbm,
    sea_hbm,
    atm_out,
    ocn,
    sea_share,
    forcing,
    state,
    halo,
    edge_own,
    edge_mate,
    edge,
    ocn_top,
    owner_ref,
    mask,
    coef,
    air,
    sea,
    cor,
    air_f32,
    sea_f32,
    air_left,
    sea_left,
    top,
    push,
    surf,
    acc,
    part,
    gathered,
    spread,
    load_sem,
    halo_send,
    halo_recv,
    part_send,
    part_recv,
    spread_send,
    spread_recv,
    edge_send,
    edge_recv,
    mate_send,
    mate_recv,
):
    me = lax.axis_index("member")
    tile = lax.axis_index("tile")
    rows, lev, lon = state.shape[2:]
    olev = ocn.shape[2] // rows
    halves = lon // 128
    last_row = rows - 1
    air_pad = -(-lev // 16) * 16
    sea_pad = -(-olev // 16) * 16
    has_south = tile > 0
    has_north = tile < tiles - 1
    early = jnp.logical_and(has_south, has_north)
    late = jnp.logical_not(early)

    barrier = pltpu.get_barrier_semaphore()

    @pl.loop(1, members)
    def _(d):
        pl.semaphore_signal(
            barrier, inc=1, device_id=(lax.rem(me + d, members), tile), device_id_type=MESH
        )

    @pl.when(has_south)
    def _():
        pl.semaphore_signal(barrier, inc=1, device_id=(me, tile - 1), device_id_type=MESH)

    @pl.when(has_north)
    def _():
        pl.semaphore_signal(barrier, inc=1, device_id=(me, tile + 1), device_id_type=MESH)

    loads = [pltpu.make_async_copy(ocn_hbm.at[f, 0:rows], ocn_top.at[i], load_sem.at[i]) for i, f in enumerate((0, 2, 3))]
    loads += [pltpu.make_async_copy(atm_hbm.at[0, f], state.at[0, f], load_sem.at[3 + f]) for f in range(4)]
    loads += [
        pltpu.make_async_copy(mask_hbm, mask, load_sem.at[7]),
        pltpu.make_async_copy(owner_hbm, owner_ref, load_sem.at[8]),
        pltpu.make_async_copy(coef_hbm, coef, load_sem.at[9]),
        pltpu.make_async_copy(air_hbm, air, load_sem.at[10]),
        pltpu.make_async_copy(sea_hbm, sea, load_sem.at[11]),
    ]
    loads += [
        pltpu.make_async_copy(ocn_hbm.at[:, :, pl.ds(128 * h, 128)], ocn.at[:, h], load_sem.at[12 + h])
        for h in range(halves)
    ]
    for load in loads:
        load.start()

    def to_south(source, k, f):
        return pltpu.make_async_remote_copy(
            src_ref=source,
            dst_ref=halo.at[k, 1, f],
            send_sem=halo_send.at[k, 0, f],
            recv_sem=halo_recv.at[k, 1, f],
            device_id=(me, tile - 1),
            device_id_type=MESH,
        )

    def to_north(source, k, f):
        return pltpu.make_async_remote_copy(
            src_ref=source,
            dst_ref=halo.at[k, 0, f],
            send_sem=halo_send.at[k, 1, f],
            recv_sem=halo_recv.at[k, 0, f],
            device_id=(me, tile + 1),
            device_id_type=MESH,
        )

    half = members // 2
    mine = lax.rem(me, half)
    base = me - mine

    def mate_copy():
        return pltpu.make_async_remote_copy(
            src_ref=edge_own,
            dst_ref=edge_mate,
            send_sem=mate_send.at[0],
            recv_sem=mate_recv.at[0],
            device_id=(lax.rem(me + half, members), tile),
            device_id_type=MESH,
        )

    def edge_copy(d):
        return pltpu.make_async_remote_copy(
            src_ref=edge.at[mine],
            dst_ref=edge.at[mine],
            send_sem=edge_send.at[0],
            recv_sem=edge_recv.at[0],
            device_id=(base + lax.rem(mine + d, half), tile),
            device_id_type=MESH,
        )

    def all_edges():
        whole = edge.at[pl.ds(0, half - 1)]
        return pltpu.make_async_remote_copy(
            src_ref=whole,
            dst_ref=whole,
            send_sem=edge_send.at[0],
            recv_sem=edge_recv.at[0],
            device_id=(base + lax.rem(mine + 1, half), tile),
            device_id_type=MESH,
        )

    block = part.shape[2]

    def pieces():
        for f in range(4):
            for half in range(2):
                for group in range(2):
                    index = (f * 2 + half) * 2 + group
                    place = (index * 4 // block, slice(index * 4 % block, index * 4 % block + 4))
                    yield f, slice(128 * half, 128 * half + 128), slice(4 * group, 4 * group + 4), place

    def part_copy(i, d):
        target = lax.rem(me + d, members)
        return pltpu.make_async_remote_copy(
            src_ref=part.at[i, target],
            dst_ref=gathered.at[i, d - 1],
            send_sem=part_send.at[i],
            recv_sem=part_recv.at[i],
            device_id=(target, tile),
            device_id_type=MESH,
        )

    def spread_copy(i, d):
        target = lax.rem(me + d, members)
        return pltpu.make_async_remote_copy(
            src_ref=spread.at[i, me],
            dst_ref=spread.at[i, me],
            send_sem=spread_send.at[i],
            recv_sem=spread_recv.at[i],
            device_id=(target, tile),
            device_id_type=MESH,
        )

    def all_pieces(ref, i, send, recv):
        whole = ref.at[i, pl.ds(0, members - 1)]
        return pltpu.make_async_remote_copy(
            src_ref=whole,
            dst_ref=whole,
            send_sem=send.at[i],
            recv_sem=recv.at[i],
            device_id=(lax.rem(me + 1, members), tile),
            device_id_type=MESH,
        )

    def sum_start(i, values):
        for f, cols, lines, (slot, at) in pieces():
            part[i, slot, at, :] = values[f][lines, cols]

        for d in sorted(range(1, members), key=lambda d: (abs(d - 3 * members // 4) > 1, abs(d - members // 2))):
            part_copy(i, d).start()

    def sum_middle(i):
        all_pieces(gathered, i, part_send, part_recv).wait_recv()
        total = part[i, me]
        for d in range(members - 1):
            total = total + gathered[i, d]
        spread[i, me] = total

        for d in sorted(range(1, members), key=lambda d: (abs(d - 3 * members // 4) > 1, abs(d - members // 2))):
            spread_copy(i, d).start()

    def sum_finish(i, out_ref, fields):
        all_pieces(spread, i, spread_send, spread_recv).wait_recv()
        for f, cols, lines, (slot, at) in pieces():
            if f < fields:
                out_ref[f, lines, cols] = spread[i, slot, at, :]

    def sum_drain(i):
        all_pieces(gathered, i, part_send, part_recv).wait_send()
        all_pieces(spread, i, spread_send, spread_recv).wait_send()

    for load in loads[:3] + loads[8:9]:
        load.wait()
    owned = jnp.broadcast_to(owner_ref[...], (rows, lon)) == me
    tops = [jnp.where(owned, ocn_top[i], 0.0) for i in range(3)]
    pl.semaphore_wait(
        barrier, members - 1 + has_south.astype(jnp.int32) + has_north.astype(jnp.int32)
    )

    sum_start(0, tops + [jnp.zeros((rows, lon), jnp.float32)])
    for f in range(4):

        @pl.when(has_south)
        def _():
            to_south(atm_hbm.at[0, f, 0], 0, f).start()

        @pl.when(has_north)
        def _():
            to_north(atm_hbm.at[0, f, last_row], 0, f).start()

    @pl.when(jnp.logical_not(has_south))
    def _():
        @pl.loop(0, NSUB)
        def _(k):
            for f in range(4):
                halo[k, 0, f] = jnp.zeros((lev, lon), jnp.float32)

    @pl.when(jnp.logical_not(has_north))
    def _():
        @pl.loop(0, NSUB)
        def _(k):
            for f in range(4):
                halo[k, 1, f] = jnp.zeros((lev, lon), jnp.float32)

    for load in loads[9:12]:
        load.wait()
    cor[...] = coriolis_rows(tile, tiles, rows, lon)
    stacked_left(air[...], air_f32, air_pad)
    stacked_left(sea[...], sea_f32, sea_pad)
    air_left[...] = air_f32[...].astype(jnp.bfloat16)
    sea_left[...] = sea_f32[...].astype(jnp.bfloat16)

    def fluxes():
        east = top[2] - surf[1]
        north = top[3] - surf[2]
        factor = surf[3] * jnp.sqrt(1.0 + east * east + north * north)
        return [
            factor * (surf[0] - top[0]),
            factor * (jnp.tanh(surf[0]) - top[1]),
            factor * east,
            factor * north,
        ]

    def set_push(values):
        for f in range(4):
            push[f] = (AIR_STEP * SIGNS[f]) * values[f]

    def accumulate(values):
        for f in range(4):
            acc[f] = acc[f] + values[f]

    def advance(k, f, r, target, pushed):
        center = state[k, f, r]
        south = halo[k, 0, f] if r == 0 else state[k, f, r - 1]
        north = halo[k, 1, f] if r == last_row else state[k, f, r + 1]
        east = pltpu.roll(center, lon - 1, 1)
        west = pltpu.roll(center, 1, 1)
        spread_out = DIFFUSE * ((north + south) + (east + west)) + (1.0 - 4.0 * DIFFUSE) * center
        if f < 2:
            flow = state[k, 2, r] * (east - west) + state[k, 3, r] * (north - south)
            moved = spread_out - (0.5 * ADVECT_RATE) * flow
        else:
            turn = cor[r : r + 1, :]
            turn = turn if f == 2 else -turn
            moved = spread_out + turn * state[k, 5 - f, r]
        mixed = mix_levels(air_left[...], moved, air_pad)
        target[f, r] = mixed
        if pushed:
            push_row(f, r, target, mixed[0:1, :])

    def push_row(f, r, target, line):
        surface = line + push[f, r : r + 1, :]
        target[f, r, 0:1, :] = surface
        top[f, r : r + 1, :] = surface

    def interior(k, f, target, pushed):
        for r in range(1, last_row):
            advance(k, f, r, target, pushed)

    def boundary(k, f, target, pushed):
        @pl.when(has_south)
        def _():
            to_north(atm_hbm.at[0, f, 0], k, f).wait_recv()

        @pl.when(has_north)
        def _():
            to_south(atm_hbm.at[0, f, 0], k, f).wait_recv()

        advance(k, f, 0, target, pushed)
        advance(k, f, last_row, target, pushed)

    def send(k, f, target):
        @pl.when(has_south)
        def _():
            to_south(target.at[f, 0], k, f).start()

        @pl.when(has_north)
        def _():
            to_north(target.at[f, last_row], k, f).start()

    for load in loads[3:7]:
        load.wait()
    for f in range(4):
        top[f] = state[0, f, :, 0, :]
        acc[f] = jnp.zeros((rows, lon), jnp.float32)
    first = state.at[1]
    for f in range(4):
        interior(0, f, first, False)
    sum_middle(0)

    for load in loads[7:8] + loads[12:]:
        load.wait()
    wet = jnp.logical_and(owned, mask[...] == 1)
    push[0] = jnp.where(wet, 1.0, 0.0)

    def mix_ocean(f, carry):
        for r in range(rows):
            levels = pl.ds(r, olev, stride=rows)
            column = jnp.concatenate([ocn[f, h, levels, :] for h in range(halves)], axis=1)
            mixed = mix_levels(sea_left[...], column, sea_pad)
            chosen = jnp.broadcast_to(push[0, r : r + 1, :], (olev, lon)) > 0.5
            column = jnp.where(chosen, mixed, column)
            for h in range(halves):
                ocn[f, h, levels, :] = column[:, 128 * h : 128 * h + 128]
        return carry

    lax.fori_loop(0, 4, mix_ocean, 0)
    line = lax.broadcasted_iota(jnp.int32, (olev, 1), 0)
    share = SEA_STEP / (NSUB * members) * (0.5 * sea[:, 0:1] + jnp.where(line == 0, 0.5, 0.0))
    sea_share[...] = jnp.broadcast_to(share, (olev, 128))

    boundary(0, 0, first, False)
    boundary(0, 1, first, False)
    surf[3] = coef[...] * mask[...].astype(jnp.float32)
    sum_finish(0, surf, 3)
    values = fluxes()
    set_push(values)
    accumulate(values)
    for f in range(4):
        if f >= 2:
            boundary(0, f, first, False)
        for r in (0, last_row):
            push_row(f, r, first, first[f, r, 0:1, :])
        send(1, f, first)
    for f in range(4):
        for r in range(1, last_row):
            push_row(f, r, first, first[f, r, 0:1, :])

    target = state.at[2]
    values = fluxes()
    set_push(values)
    accumulate(values)
    for f in range(4):
        interior(1, f, target, True)
        boundary(1, f, target, True)
        send(2, f, target)

    target = state.at[3]
    values = fluxes()
    set_push(values)
    accumulate(values)
    line = lax.broadcasted_iota(jnp.int32, (rows, lon), 0)
    inner = jnp.logical_and(line > 0, line < last_row)
    interior(2, 0, target, True)
    for f in range(4):
        boundary(2, f, target, True)
        send(3, f, target)
        if f == 0:
            interior(2, 1, target, True)
            interior(2, 2, target, True)
        if f == 1:
            interior(2, 3, target, True)
            values = fluxes()
            ahead = [acc[g] + jnp.where(inner, values[g], 0.0) for g in range(4)]

            @pl.when(early)
            def _():
                sum_start(1, ahead)

    last = atm_out.at[0]
    values = fluxes()
    set_push(values)
    whole = [acc[f] + values[f] for f in range(4)]

    @pl.when(late)
    def _():
        sum_start(1, whole)

    @pl.when(early)
    def _():
        for f in range(4):
            edge_own[2 * f : 2 * f + 1, :] = values[f][0:1, :]
            edge_own[2 * f + 1 : 2 * f + 2, :] = values[f][last_row:rows, :]
        mate_copy().start()

    interior(3, 0, last, True)
    boundary(3, 0, last, True)

    @pl.when(early)
    def _():
        mate_copy().wait_recv()
        edge[mine] = edge_own[...] + edge_mate[...]
        for d in range(1, half):
            edge_copy(d).start()
        sum_middle(1)

    for f in range(1, 4):
        interior(3, f, last, True)
        boundary(3, f, last, True)
        if f == 1:

            @pl.when(late)
            def _():
                sum_middle(1)

    sum_finish(1, acc, 4)

    @pl.when(early)
    def _():
        all_edges().wait_recv()
        total = edge[0]
        for m in range(1, half):
            total = total + edge[m]
        for f in range(4):
            acc[f, 0:1, :] = acc[f, 0:1, :] + total[2 * f : 2 * f + 1, :]
            acc[f, last_row:rows, :] = acc[f, last_row:rows, :] + total[2 * f + 1 : 2 * f + 2, :]

    for f in range(4):
        forcing[f] = jnp.where(wet, acc[f], 0.0)

    for i in range(2):
        sum_drain(i)

    @pl.when(early)
    def _():
        all_edges().wait_send()
        mate_copy().wait_send()


    @pl.loop(0, NSUB)
    def _(k):
        for f in range(4):

            @pl.when(has_south)
            def _():
                to_south(atm_hbm.at[0, f, 0], k, f).wait_send()

            @pl.when(has_north)
            def _():
                to_north(atm_hbm.at[0, f, 0], k, f).wait_send()


def put(atmos, base, share, forcing, atmos_out, ocean_out, ocean, sem):
    fields, halves, lines, _ = base.shape
    rows = forcing.shape[1]
    copies = [pltpu.make_async_copy(atmos.at[0, f], atmos_out.at[0, f], sem.at[f]) for f in range(fields)]
    for copy in copies:
        copy.start()
    for f in range(fields):
        for h in range(halves):
            cols = slice(128 * h, 128 * h + 128)
            flux = forcing[f, :, cols]
            for level in range(lines // rows):
                at = slice(level * rows, level * rows + rows)
                ocean[f, h, at, :] = base[f, h, at, :] + share[level : level + 1, :] * flux
            copy = pltpu.make_async_copy(
                ocean.at[f, h], ocean_out.at[f, :, pl.ds(128 * h, 128)], sem.at[fields + f * halves + h]
            )
            copy.start()
            copies.append(copy)
    for copy in copies:
        copy.wait()


def shards(members, tiles, atmos_state, ocean_slots, owner_map, land_mask, transfer, air_mixing, sea_mixing):
    fields, rows, lev, lon = atmos_state.shape[1:]
    olev = ocean_slots.shape[3]
    air_pad = -(-lev // 16) * 16
    sea_pad = -(-olev // 16) * 16
    block = fields * rows * lon // 128 // members
    anywhere = pl.BlockSpec(memory_space=pltpu.MemorySpace.HBM)
    slots = ocean_slots.transpose(0, 1, 3, 2, 4).reshape(fields, olev * rows, lon)
    vmem = pl.BlockSpec(memory_space=pltpu.VMEM)
    halves = lon // 128
    base_shape = (fields, halves, olev * rows, 128)
    atmos, base, share, forcing = pl.pallas_call(
        functools.partial(kernel, members, tiles),
        out_shape=(
            jax.ShapeDtypeStruct(atmos_state.shape, jnp.float32),
            jax.ShapeDtypeStruct(base_shape, jnp.float32),
            jax.ShapeDtypeStruct((olev, 128), jnp.float32),
            jax.ShapeDtypeStruct((fields, rows, lon), jnp.float32),
        ),
        in_specs=[anywhere] * 7,
        out_specs=(vmem,) * 4,
        scratch_shapes=[
            pltpu.VMEM((NSUB, fields, rows, lev, lon), jnp.float32),
            pltpu.VMEM((NSUB, 2, fields, lev, lon), jnp.float32),
            pltpu.VMEM((2 * fields, lon), jnp.float32),
            pltpu.VMEM((2 * fields, lon), jnp.float32),
            pltpu.VMEM((members // 2, 2 * fields, lon), jnp.float32),
            pltpu.VMEM((3, rows, lon), jnp.float32),
            pltpu.VMEM((1, 1), jnp.int32),
            pltpu.VMEM((rows, lon), jnp.int32),
            pltpu.VMEM((rows, lon), jnp.float32),
            pltpu.VMEM((lev, lev), jnp.float32),
            pltpu.VMEM((olev, olev), jnp.float32),
            pltpu.VMEM((rows, lon), jnp.float32),
            pltpu.VMEM((lev, 3 * air_pad), jnp.float32),
            pltpu.VMEM((olev, 3 * sea_pad), jnp.float32),
            pltpu.VMEM((lev, 3 * air_pad), jnp.bfloat16),
            pltpu.VMEM((olev, 3 * sea_pad), jnp.bfloat16),
            pltpu.VMEM((fields, rows, lon), jnp.float32),
            pltpu.VMEM((fields, rows, lon), jnp.float32),
            pltpu.VMEM((fields, rows, lon), jnp.float32),
            pltpu.VMEM((fields, rows, lon), jnp.float32),
            pltpu.VMEM((2, members, block, 128), jnp.float32),
            pltpu.VMEM((2, members - 1, block, 128), jnp.float32),
            pltpu.VMEM((2, members, block, 128), jnp.float32),
            pltpu.SemaphoreType.DMA((12 + lon // 128,)),
            pltpu.SemaphoreType.DMA((NSUB, 2, fields)),
            pltpu.SemaphoreType.DMA((NSUB, 2, fields)),
            pltpu.SemaphoreType.DMA((2,)),
            pltpu.SemaphoreType.DMA((2,)),
            pltpu.SemaphoreType.DMA((2,)),
            pltpu.SemaphoreType.DMA((2,)),
            pltpu.SemaphoreType.DMA((1,)),
            pltpu.SemaphoreType.DMA((1,)),
            pltpu.SemaphoreType.DMA((1,)),
            pltpu.SemaphoreType.DMA((1,)),
        ],
        compiler_params=pltpu.CompilerParams(
            collective_id=0, has_side_effects=True, vmem_limit_bytes=40 * 1024 * 1024
        ),
        name="window",
    )(
        owner_map.reshape(1, 1),
        *[
            pltpu.with_memory_space_constraint(x, pltpu.MemorySpace.HBM)
            for x in (atmos_state, slots, land_mask, transfer, air_mixing, sea_mixing)
        ],
    )
    atmos, ocean = pl.pallas_call(
        put,
        out_shape=(
            jax.ShapeDtypeStruct(atmos_state.shape, jnp.float32),
            jax.ShapeDtypeStruct(slots.shape, jnp.float32),
        ),
        in_specs=[vmem] * 4,
        out_specs=(anywhere, anywhere),
        scratch_shapes=[
            pltpu.VMEM(base_shape, jnp.float32),
            pltpu.SemaphoreType.DMA((fields * (1 + halves),)),
        ],
        compiler_params=pltpu.CompilerParams(vmem_limit_bytes=8 * 1024 * 1024),
        name="put",
    )(atmos, base, share, forcing)
    ocean = ocean.reshape(1, fields, olev, rows, lon).transpose(0, 1, 3, 2, 4)
    return atmos, ocean


def solution(mesh):
    placed = (
        P("member", None, "tile", None, None),
        P("member", None, "tile", None, None),
        P("tile"),
        P("tile", None),
        P("tile", None),
        P(),
        P(),
    )
    return jax.shard_map(
        functools.partial(shards, mesh.shape["member"], mesh.shape["tile"]),
        mesh=mesh,
        in_specs=placed,
        out_specs=(P("member", None, "tile", None, None), P("member", None, "tile", None, None)),
        check_vma=False,
    )
```

```python
import functools

import jax
import jax.numpy as jnp
import numpy as np
from jax import lax
from jax.experimental import pallas as pl
from jax.experimental.pallas import tpu as pltpu
from jax.sharding import PartitionSpec as P

NSUB = 4
DIFFUSE = 0.2
ADVECT_RATE = 0.15
CORIOLIS_MAX = 0.2
AIR_STEP = 0.05
SEA_STEP = 0.25
MESH = pl.DeviceIdType.MESH
SIGNS = (1.0, 1.0, -1.0, -1.0)


def stacked_left(mix, out_ref, pad):
    size = mix.shape[0]
    row = lax.broadcasted_iota(jnp.int32, (size, size), 0)
    col = lax.broadcasted_iota(jnp.int32, (size, size), 1)
    whole = 0.5 * mix + jnp.where(row == col, 0.5, 0.0)
    high = whole.astype(jnp.bfloat16).astype(jnp.float32)
    low = whole - high
    out_ref[...] = jnp.zeros_like(out_ref)
    out_ref[:, 0:size] = high
    out_ref[:, pad : pad + size] = high
    out_ref[:, 2 * pad : 2 * pad + size] = low


def stacked_right(cells, pad):
    size, width = cells.shape
    if pad > size:
        cells = jnp.concatenate([cells, jnp.zeros((pad - size, width), jnp.float32)], axis=0)
    high = cells.astype(jnp.bfloat16)
    low = (cells - high.astype(jnp.float32)).astype(jnp.bfloat16)
    return jnp.concatenate([high, low, high], axis=0)


def coriolis_rows(tile, tiles, rows, width):
    total = rows * tiles
    sin_tile = jnp.float32(0.0)
    cos_tile = jnp.float32(0.0)
    for index in range(tiles):
        angle = np.pi * (index * rows / total - 0.5)
        sin_tile = jnp.where(tile == index, jnp.float32(CORIOLIS_MAX * np.sin(angle)), sin_tile)
        cos_tile = jnp.where(tile == index, jnp.float32(CORIOLIS_MAX * np.cos(angle)), cos_tile)
    line = lax.broadcasted_iota(jnp.int32, (rows, width), 0)
    sin_row = jnp.zeros((rows, width), jnp.float32)
    cos_row = jnp.zeros((rows, width), jnp.float32)
    for index in range(rows):
        angle = np.pi * (index + 0.5) / total
        sin_row = jnp.where(line == index, jnp.float32(np.sin(angle)), sin_row)
        cos_row = jnp.where(line == index, jnp.float32(np.cos(angle)), cos_row)
    return sin_tile * cos_row + cos_tile * sin_row


def mix_levels(left, cells, pad):
    return jnp.dot(left, stacked_right(cells, pad), preferred_element_type=jnp.float32)


def kernel(
    members,
    tiles,
    owner_hbm,
    atm_hbm,
    ocn_hbm,
    mask_hbm,
    coef_hbm,
    air_hbm,
    sea_hbm,
    atm_out,
    ocn,
    sea_share,
    forcing,
    state,
    halo,
    edge_own,
    edge_mate,
    edge,
    ocn_top,
    owner_ref,
    mask,
    coef,
    air,
    sea,
    cor,
    air_f32,
    sea_f32,
    air_left,
    sea_left,
    top,
    push,
    surf,
    acc,
    part,
    gathered,
    spread,
    load_sem,
    halo_send,
    halo_recv,
    part_send,
    part_recv,
    spread_send,
    spread_recv,
    edge_send,
    edge_recv,
    mate_send,
    mate_recv,
):
    me = lax.axis_index("member")
    tile = lax.axis_index("tile")
    rows, lev, lon = state.shape[2:]
    olev = ocn.shape[2] // rows
    halves = lon // 128
    last_row = rows - 1
    air_pad = -(-lev // 16) * 16
    sea_pad = -(-olev // 16) * 16
    has_south = tile > 0
    has_north = tile < tiles - 1
    early = jnp.logical_and(has_south, has_north)
    late = jnp.logical_not(early)

    barrier = pltpu.get_barrier_semaphore()

    @pl.loop(1, members)
    def _(d):
        pl.semaphore_signal(
            barrier, inc=1, device_id=(lax.rem(me + d, members), tile), device_id_type=MESH
        )

    @pl.when(has_south)
    def _():
        pl.semaphore_signal(barrier, inc=1, device_id=(me, tile - 1), device_id_type=MESH)

    @pl.when(has_north)
    def _():
        pl.semaphore_signal(barrier, inc=1, device_id=(me, tile + 1), device_id_type=MESH)

    loads = [pltpu.make_async_copy(ocn_hbm.at[f, 0:rows], ocn_top.at[i], load_sem.at[i]) for i, f in enumerate((0, 2, 3))]
    loads += [pltpu.make_async_copy(atm_hbm.at[0, f], state.at[0, f], load_sem.at[3 + f]) for f in range(4)]
    loads += [
        pltpu.make_async_copy(mask_hbm, mask, load_sem.at[7]),
        pltpu.make_async_copy(owner_hbm, owner_ref, load_sem.at[8]),
        pltpu.make_async_copy(coef_hbm, coef, load_sem.at[9]),
        pltpu.make_async_copy(air_hbm, air, load_sem.at[10]),
        pltpu.make_async_copy(sea_hbm, sea, load_sem.at[11]),
    ]
    loads += [
        pltpu.make_async_copy(ocn_hbm.at[:, :, pl.ds(128 * h, 128)], ocn.at[:, h], load_sem.at[12 + h])
        for h in range(halves)
    ]
    for load in loads:
        load.start()

    def to_south(source, k, f):
        return pltpu.make_async_remote_copy(
            src_ref=source,
            dst_ref=halo.at[k, 1, f],
            send_sem=halo_send.at[k, 0, f],
            recv_sem=halo_recv.at[k, 1, f],
            device_id=(me, tile - 1),
            device_id_type=MESH,
        )

    def to_north(source, k, f):
        return pltpu.make_async_remote_copy(
            src_ref=source,
            dst_ref=halo.at[k, 0, f],
            send_sem=halo_send.at[k, 1, f],
            recv_sem=halo_recv.at[k, 0, f],
            device_id=(me, tile + 1),
            device_id_type=MESH,
        )

    half = members // 2
    mine = lax.rem(me, half)
    base = me - mine

    def mate_copy():
        return pltpu.make_async_remote_copy(
            src_ref=edge_own,
            dst_ref=edge_mate,
            send_sem=mate_send.at[0],
            recv_sem=mate_recv.at[0],
            device_id=(lax.rem(me + half, members), tile),
            device_id_type=MESH,
        )

    def edge_copy(d):
        return pltpu.make_async_remote_copy(
            src_ref=edge.at[mine],
            dst_ref=edge.at[mine],
            send_sem=edge_send.at[0],
            recv_sem=edge_recv.at[0],
            device_id=(base + lax.rem(mine + d, half), tile),
            device_id_type=MESH,
        )

    def all_edges():
        whole = edge.at[pl.ds(0, half - 1)]
        return pltpu.make_async_remote_copy(
            src_ref=whole,
            dst_ref=whole,
            send_sem=edge_send.at[0],
            recv_sem=edge_recv.at[0],
            device_id=(base + lax.rem(mine + 1, half), tile),
            device_id_type=MESH,
        )

    block = part.shape[2]

    def pieces():
        for f in range(4):
            for half in range(2):
                for group in range(2):
                    index = (f * 2 + half) * 2 + group
                    place = (index * 4 // block, slice(index * 4 % block, index * 4 % block + 4))
                    yield f, slice(128 * half, 128 * half + 128), slice(4 * group, 4 * group + 4), place

    def part_copy(i, d):
        target = lax.rem(me + d, members)
        return pltpu.make_async_remote_copy(
            src_ref=part.at[i, target],
            dst_ref=gathered.at[i, d - 1],
            send_sem=part_send.at[i],
            recv_sem=part_recv.at[i],
            device_id=(target, tile),
            device_id_type=MESH,
        )

    def spread_copy(i, d):
        target = lax.rem(me + d, members)
        return pltpu.make_async_remote_copy(
            src_ref=spread.at[i, me],
            dst_ref=spread.at[i, me],
            send_sem=spread_send.at[i],
            recv_sem=spread_recv.at[i],
            device_id=(target, tile),
            device_id_type=MESH,
        )

    def all_pieces(ref, i, send, recv):
        whole = ref.at[i, pl.ds(0, members - 1)]
        return pltpu.make_async_remote_copy(
            src_ref=whole,
            dst_ref=whole,
            send_sem=send.at[i],
            recv_sem=recv.at[i],
            device_id=(lax.rem(me + 1, members), tile),
            device_id_type=MESH,
        )

    def sum_start(i, values):
        for f, cols, lines, (slot, at) in pieces():
            part[i, slot, at, :] = values[f][lines, cols]

        for d in sorted(range(1, members), key=lambda d: (abs(d - 3 * members // 4) > 1, abs(d - members // 2))):
            part_copy(i, d).start()

    def sum_middle(i):
        all_pieces(gathered, i, part_send, part_recv).wait_recv()
        total = part[i, me]
        for d in range(members - 1):
            total = total + gathered[i, d]
        spread[i, me] = total

        for d in sorted(range(1, members), key=lambda d: (abs(d - 3 * members // 4) > 1, abs(d - members // 2))):
            spread_copy(i, d).start()

    def sum_finish(i, out_ref, fields):
        all_pieces(spread, i, spread_send, spread_recv).wait_recv()
        for f, cols, lines, (slot, at) in pieces():
            if f < fields:
                out_ref[f, lines, cols] = spread[i, slot, at, :]

    def sum_drain(i):
        all_pieces(gathered, i, part_send, part_recv).wait_send()
        all_pieces(spread, i, spread_send, spread_recv).wait_send()

    for load in loads[:3] + loads[8:9]:
        load.wait()
    owned = jnp.broadcast_to(owner_ref[...], (rows, lon)) == me
    tops = [jnp.where(owned, ocn_top[i], 0.0) for i in range(3)]
    pl.semaphore_wait(
        barrier, members - 1 + has_south.astype(jnp.int32) + has_north.astype(jnp.int32)
    )

    sum_start(0, tops + [jnp.zeros((rows, lon), jnp.float32)])
    for f in range(4):

        @pl.when(has_south)
        def _():
            to_south(atm_hbm.at[0, f, 0], 0, f).start()

        @pl.when(has_north)
        def _():
            to_north(atm_hbm.at[0, f, last_row], 0, f).start()

    @pl.when(jnp.logical_not(has_south))
    def _():
        @pl.loop(0, NSUB)
        def _(k):
            for f in range(4):
                halo[k, 0, f] = jnp.zeros((lev, lon), jnp.float32)

    @pl.when(jnp.logical_not(has_north))
    def _():
        @pl.loop(0, NSUB)
        def _(k):
            for f in range(4):
                halo[k, 1, f] = jnp.zeros((lev, lon), jnp.float32)

    for load in loads[9:12]:
        load.wait()
    cor[...] = coriolis_rows(tile, tiles, rows, lon)
    stacked_left(air[...], air_f32, air_pad)
    stacked_left(sea[...], sea_f32, sea_pad)
    air_left[...] = air_f32[...].astype(jnp.bfloat16)
    sea_left[...] = sea_f32[...].astype(jnp.bfloat16)

    def fluxes():
        east = top[2] - surf[1]
        north = top[3] - surf[2]
        factor = surf[3] * jnp.sqrt(1.0 + east * east + north * north)
        return [
            factor * (surf[0] - top[0]),
            factor * (jnp.tanh(surf[0]) - top[1]),
            factor * east,
            factor * north,
        ]

    def set_push(values):
        for f in range(4):
            push[f] = (AIR_STEP * SIGNS[f]) * values[f]

    def accumulate(values):
        for f in range(4):
            acc[f] = acc[f] + values[f]

    def advance(k, f, r, target, pushed):
        center = state[k, f, r]
        south = halo[k, 0, f] if r == 0 else state[k, f, r - 1]
        north = halo[k, 1, f] if r == last_row else state[k, f, r + 1]
        east = pltpu.roll(center, lon - 1, 1)
        west = pltpu.roll(center, 1, 1)
        spread_out = DIFFUSE * ((north + south) + (east + west)) + (1.0 - 4.0 * DIFFUSE) * center
        if f < 2:
            flow = state[k, 2, r] * (east - west) + state[k, 3, r] * (north - south)
            moved = spread_out - (0.5 * ADVECT_RATE) * flow
        else:
            turn = cor[r : r + 1, :]
            turn = turn if f == 2 else -turn
            moved = spread_out + turn * state[k, 5 - f, r]
        mixed = mix_levels(air_left[...], moved, air_pad)
        target[f, r] = mixed
        if pushed:
            push_row(f, r, target, mixed[0:1, :])

    def push_row(f, r, target, line):
        surface = line + push[f, r : r + 1, :]
        target[f, r, 0:1, :] = surface
        top[f, r : r + 1, :] = surface

    def interior(k, f, target, pushed):
        for r in range(1, last_row):
            advance(k, f, r, target, pushed)

    def boundary(k, f, target, pushed):
        @pl.when(has_south)
        def _():
            to_north(atm_hbm.at[0, f, 0], k, f).wait_recv()

        @pl.when(has_north)
        def _():
            to_south(atm_hbm.at[0, f, 0], k, f).wait_recv()

        advance(k, f, 0, target, pushed)
        advance(k, f, last_row, target, pushed)

    def send(k, f, target):
        @pl.when(has_south)
        def _():
            to_south(target.at[f, 0], k, f).start()

        @pl.when(has_north)
        def _():
            to_north(target.at[f, last_row], k, f).start()

    for load in loads[3:7]:
        load.wait()
    for f in range(4):
        top[f] = state[0, f, :, 0, :]
        acc[f] = jnp.zeros((rows, lon), jnp.float32)
    first = state.at[1]
    for f in range(4):
        interior(0, f, first, False)
    sum_middle(0)

    for load in loads[7:8] + loads[12:]:
        load.wait()
    wet = jnp.logical_and(owned, mask[...] == 1)
    push[0] = jnp.where(wet, 1.0, 0.0)

    def mix_ocean(f, carry):
        for r in range(rows):
            levels = pl.ds(r, olev, stride=rows)
            column = jnp.concatenate([ocn[f, h, levels, :] for h in range(halves)], axis=1)
            mixed = mix_levels(sea_left[...], column, sea_pad)
            chosen = jnp.broadcast_to(push[0, r : r + 1, :], (olev, lon)) > 0.5
            column = jnp.where(chosen, mixed, column)
            for h in range(halves):
                ocn[f, h, levels, :] = column[:, 128 * h : 128 * h + 128]
        return carry

    lax.fori_loop(0, 4, mix_ocean, 0)
    line = lax.broadcasted_iota(jnp.int32, (olev, 1), 0)
    share = SEA_STEP / (NSUB * members) * (0.5 * sea[:, 0:1] + jnp.where(line == 0, 0.5, 0.0))
    sea_share[...] = jnp.broadcast_to(share, (olev, 128))

    boundary(0, 0, first, False)
    boundary(0, 1, first, False)
    surf[3] = coef[...] * mask[...].astype(jnp.float32)
    sum_finish(0, surf, 3)
    values = fluxes()
    set_push(values)
    accumulate(values)
    for f in range(4):
        if f >= 2:
            boundary(0, f, first, False)
        for r in (0, last_row):
            push_row(f, r, first, first[f, r, 0:1, :])
        send(1, f, first)
    for f in range(4):
        for r in range(1, last_row):
            push_row(f, r, first, first[f, r, 0:1, :])

    target = state.at[2]
    values = fluxes()
    set_push(values)
    accumulate(values)
    for f in range(4):
        interior(1, f, target, True)
        boundary(1, f, target, True)
        send(2, f, target)

    target = state.at[3]
    values = fluxes()
    set_push(values)
    accumulate(values)
    line = lax.broadcasted_iota(jnp.int32, (rows, lon), 0)
    inner = jnp.logical_and(line > 0, line < last_row)
    interior(2, 0, target, True)
    for f in range(4):
        boundary(2, f, target, True)
        send(3, f, target)
        if f == 0:
            interior(2, 1, target, True)
            interior(2, 2, target, True)
        if f == 1:
            interior(2, 3, target, True)
            values = fluxes()
            ahead = [acc[g] + jnp.where(inner, values[g], 0.0) for g in range(4)]

            @pl.when(early)
            def _():
                sum_start(1, ahead)

    def rows_left(k):
        for f in range(4):

            @pl.when(has_south)
            def _():
                to_south(atm_hbm.at[0, f, 0], k, f).wait_send()

            @pl.when(has_north)
            def _():
                to_north(atm_hbm.at[0, f, 0], k, f).wait_send()

    last = atm_out.at[0]
    values = fluxes()
    set_push(values)
    whole = [acc[f] + values[f] for f in range(4)]

    @pl.when(late)
    def _():
        sum_start(1, whole)

    @pl.when(early)
    def _():
        for f in range(4):
            edge_own[2 * f : 2 * f + 1, :] = values[f][0:1, :]
            edge_own[2 * f + 1 : 2 * f + 2, :] = values[f][last_row:rows, :]
        mate_copy().start()

    interior(3, 0, last, True)
    boundary(3, 0, last, True)

    @pl.when(early)
    def _():
        mate_copy().wait_recv()
        edge[mine] = edge_own[...] + edge_mate[...]
        for d in range(1, half):
            edge_copy(d).start()
        sum_middle(1)

    for f in range(1, 4):
        interior(3, f, last, True)
        boundary(3, f, last, True)
        if f == 1:

            @pl.when(late)
            def _():
                sum_middle(1)

            for k in range(NSUB - 1):
                rows_left(k)
            sum_drain(0)

    sum_finish(1, acc, 4)

    @pl.when(early)
    def _():
        all_edges().wait_recv()
        total = edge[0]
        for m in range(1, half):
            total = total + edge[m]
        for f in range(4):
            acc[f, 0:1, :] = acc[f, 0:1, :] + total[2 * f : 2 * f + 1, :]
            acc[f, last_row:rows, :] = acc[f, last_row:rows, :] + total[2 * f + 1 : 2 * f + 2, :]

    for f in range(4):
        forcing[f] = jnp.where(wet, acc[f], 0.0)

    sum_drain(1)

    @pl.when(early)
    def _():
        all_edges().wait_send()
        mate_copy().wait_send()


    rows_left(NSUB - 1)


def put(atmos, base, share, forcing, atmos_out, ocean_out, ocean, sem):
    fields, halves, lines, _ = base.shape
    rows = forcing.shape[1]
    copies = [pltpu.make_async_copy(atmos.at[0, f], atmos_out.at[0, f], sem.at[f]) for f in range(fields)]
    for copy in copies:
        copy.start()
    for f in range(fields):
        for h in range(halves):
            cols = slice(128 * h, 128 * h + 128)
            flux = forcing[f, :, cols]
            for level in range(lines // rows):
                at = slice(level * rows, level * rows + rows)
                ocean[f, at, cols] = base[f, h, at, :] + share[level : level + 1, :] * flux
        copy = pltpu.make_async_copy(ocean.at[f], ocean_out.at[f], sem.at[fields + f])
        copy.start()
        copies.append(copy)
    for copy in copies:
        copy.wait()


def shards(members, tiles, atmos_state, ocean_slots, owner_map, land_mask, transfer, air_mixing, sea_mixing):
    fields, rows, lev, lon = atmos_state.shape[1:]
    olev = ocean_slots.shape[3]
    air_pad = -(-lev // 16) * 16
    sea_pad = -(-olev // 16) * 16
    block = fields * rows * lon // 128 // members
    anywhere = pl.BlockSpec(memory_space=pltpu.MemorySpace.HBM)
    slots = ocean_slots.transpose(0, 1, 3, 2, 4).reshape(fields, olev * rows, lon)
    vmem = pl.BlockSpec(memory_space=pltpu.VMEM)
    halves = lon // 128
    base_shape = (fields, halves, olev * rows, 128)
    atmos, base, share, forcing = pl.pallas_call(
        functools.partial(kernel, members, tiles),
        out_shape=(
            jax.ShapeDtypeStruct(atmos_state.shape, jnp.float32),
            jax.ShapeDtypeStruct(base_shape, jnp.float32),
            jax.ShapeDtypeStruct((olev, 128), jnp.float32),
            jax.ShapeDtypeStruct((fields, rows, lon), jnp.float32),
        ),
        in_specs=[anywhere] * 7,
        out_specs=(vmem,) * 4,
        scratch_shapes=[
            pltpu.VMEM((NSUB, fields, rows, lev, lon), jnp.float32),
            pltpu.VMEM((NSUB, 2, fields, lev, lon), jnp.float32),
            pltpu.VMEM((2 * fields, lon), jnp.float32),
            pltpu.VMEM((2 * fields, lon), jnp.float32),
            pltpu.VMEM((members // 2, 2 * fields, lon), jnp.float32),
            pltpu.VMEM((3, rows, lon), jnp.float32),
            pltpu.VMEM((1, 1), jnp.int32),
            pltpu.VMEM((rows, lon), jnp.int32),
            pltpu.VMEM((rows, lon), jnp.float32),
            pltpu.VMEM((lev, lev), jnp.float32),
            pltpu.VMEM((olev, olev), jnp.float32),
            pltpu.VMEM((rows, lon), jnp.float32),
            pltpu.VMEM((lev, 3 * air_pad), jnp.float32),
            pltpu.VMEM((olev, 3 * sea_pad), jnp.float32),
            pltpu.VMEM((lev, 3 * air_pad), jnp.bfloat16),
            pltpu.VMEM((olev, 3 * sea_pad), jnp.bfloat16),
            pltpu.VMEM((fields, rows, lon), jnp.float32),
            pltpu.VMEM((fields, rows, lon), jnp.float32),
            pltpu.VMEM((fields, rows, lon), jnp.float32),
            pltpu.VMEM((fields, rows, lon), jnp.float32),
            pltpu.VMEM((2, members, block, 128), jnp.float32),
            pltpu.VMEM((2, members - 1, block, 128), jnp.float32),
            pltpu.VMEM((2, members, block, 128), jnp.float32),
            pltpu.SemaphoreType.DMA((12 + lon // 128,)),
            pltpu.SemaphoreType.DMA((NSUB, 2, fields)),
            pltpu.SemaphoreType.DMA((NSUB, 2, fields)),
            pltpu.SemaphoreType.DMA((2,)),
            pltpu.SemaphoreType.DMA((2,)),
            pltpu.SemaphoreType.DMA((2,)),
            pltpu.SemaphoreType.DMA((2,)),
            pltpu.SemaphoreType.DMA((1,)),
            pltpu.SemaphoreType.DMA((1,)),
            pltpu.SemaphoreType.DMA((1,)),
            pltpu.SemaphoreType.DMA((1,)),
        ],
        compiler_params=pltpu.CompilerParams(
            collective_id=0, has_side_effects=True, vmem_limit_bytes=40 * 1024 * 1024
        ),
        name="window",
    )(
        owner_map.reshape(1, 1),
        *[
            pltpu.with_memory_space_constraint(x, pltpu.MemorySpace.HBM)
            for x in (atmos_state, slots, land_mask, transfer, air_mixing, sea_mixing)
        ],
    )
    atmos, ocean = pl.pallas_call(
        put,
        out_shape=(
            jax.ShapeDtypeStruct(atmos_state.shape, jnp.float32),
            jax.ShapeDtypeStruct(slots.shape, jnp.float32),
        ),
        in_specs=[vmem] * 4,
        out_specs=(anywhere, anywhere),
        scratch_shapes=[
            pltpu.VMEM(slots.shape, jnp.float32),
            pltpu.SemaphoreType.DMA((2 * fields,)),
        ],
        compiler_params=pltpu.CompilerParams(vmem_limit_bytes=8 * 1024 * 1024),
        name="put",
    )(atmos, base, share, forcing)
    ocean = ocean.reshape(1, fields, olev, rows, lon).transpose(0, 1, 3, 2, 4)
    return atmos, ocean


def solution(mesh):
    placed = (
        P("member", None, "tile", None, None),
        P("member", None, "tile", None, None),
        P("tile"),
        P("tile", None),
        P("tile", None),
        P(),
        P(),
    )
    return jax.shard_map(
        functools.partial(shards, mesh.shape["member"], mesh.shape["tile"]),
        mesh=mesh,
        in_specs=placed,
        out_specs=(P("member", None, "tile", None, None), P("member", None, "tile", None, None)),
        check_vma=False,
    )
```
